512 devices in a mesh: head: 16 (over y, z_hi), seq: 32 (over x, z_lo, core).
Axes of the slice: x: 4, y: 8, z: 8 (z_hi: 2, z_lo: 4; z = z_hi * 4 + z_lo), core: 2. Of those that a mesh axis runs over, the one named last changes fastest.
Arguments:
- queries: bfloat16 [1, 32768, 8192], P(None, 'seq', 'head'), may hold values from -6 to 6
- keys: bfloat16 [1, 32768, 8192], P(None, 'seq', 'head'), may hold values from -6 to 6
- values: bfloat16 [1, 32768, 8192], P(None, 'seq', 'head'), may hold values from -60 to 60
- decay_rate: float32 [64], P('head'), may hold values from 1.5258789e-07 to 0.03
- norm_gain: float32 [8192], P('head'), may hold values from 0.25 to 1.75
- offsets: int32 [1], replicated, may hold values from 0 to 31
Outputs:
- normed: bfloat16 [1, 32768, 8192], P(None, 'seq', 'head')
The draws below stay inside these ranges and needn't reach their ends.
All inputs are finite; a program needn't handle non-finite values.
Results may differ from the reference program's by a relative error of at most 0.0044.
Values sent between devices are 32-bit elements; how exact they have to be, the bound alone decides.
No kernel may reach another device: no remote copies, remote signals or barrier semaphores. Data moves between devices by JAX's collectives and lax.ppermute only.
A program may use at most 64 MiB of HBM per device.

```python
import math
import jax
import jax.numpy as jnp
from jax import lax

HEADS = 64
HEAD_DIM = 128
SEQS = 1
GROUP = 1024
FEATURES = 8192
LENGTH = 32768
N_SEQ = 32


def draw_values(key, part):
    head_key, noise_key = jax.random.split(jax.random.fold_in(key, 11))
    spread_level = jax.random.uniform(head_key, (HEADS,), jnp.float32)
    rising = 3.0 ** (jnp.arange(HEADS).astype(jnp.float32) / max(HEADS - 1, 1))
    noise_draw = jnp.clip(jax.random.normal(noise_key, (SEQS, LENGTH, HEADS, HEAD_DIM), jnp.float32), -6.0, 6.0)
    head_scale = 10.0 ** spread_level * rising / 3.0
    return (noise_draw * head_scale[:, None]).reshape(SEQS, LENGTH, HEADS * HEAD_DIM).astype(jnp.bfloat16)


def draw_decay_rate(key, part):
    rate_key = jax.random.fold_in(jax.random.fold_in(key, 23), 1)
    low_log = math.log(0.005 / LENGTH)
    high_log = math.log(0.03)
    spread_level = jax.random.uniform(rate_key, (HEADS,), jnp.float32)
    return jnp.exp(low_log + spread_level * (high_log - low_log)).astype(jnp.float32)


def level_of(key, dims, shards, least, top_value):
    level, own = 1.0, jax.random.fold_in(key, 6)
    for position, blocks in shards:
        heights = jnp.exp(jax.random.uniform(jax.random.fold_in(own, position), (blocks,), jnp.float32, least / len(shards), top_value / len(shards)))
        level = level * jnp.repeat(heights, dims[position] // blocks).reshape([-1 if axis == position else 1 for axis in range(len(dims))])
    return level


def centred(stream_key, extent, scale, reach, cuts=(), dtype=jnp.bfloat16):
    array = jax.random.normal(stream_key, extent, jnp.float32) * scale
    if len(cuts) > 0:
        array = level_of(stream_key, extent, cuts, -0.22, 0.18) * array
    return jnp.clip(array, min=-reach, max=reach).astype(dtype)


def setup_inputs(seed: int = 0) -> dict:
    key_list = jax.random.split(jax.random.key(seed), 7)
    return {
        "queries": centred(key_list[0], (SEQS, LENGTH, FEATURES), 1.0, 6.0, ((1, 32), (2, 16))),
        "keys": centred(key_list[1], (SEQS, LENGTH, FEATURES), 1.0, 6.0, ((1, 32), (2, 16))),
        "values": draw_values(jax.random.fold_in(key_list[6], 71), 0),
        "decay_rate": draw_decay_rate(jax.random.fold_in(key_list[6], 71), 0),
        "norm_gain": jnp.clip(1.0 + 0.15 * jax.random.normal(key_list[4], (FEATURES,), jnp.float32), 0.25, 1.75),
        "offsets": jax.random.randint(key_list[5], (SEQS,), 0, N_SEQ).astype(jnp.int32),
    }


epsilon = 1e-05

def reference(queries, keys, values, decay_rate, norm_gain, offsets):
    rates = decay_rate.astype(jnp.float32)
    places = jnp.arange(GROUP).astype(jnp.float32)
    distance = places[:, None] - places[None, :]
    within = jnp.exp(-rates[:, None, None] * jnp.maximum(distance, 0.0)[None]) * (distance >= 0.0).astype(jnp.float32)[None]
    key_scale = jnp.exp(-rates[None, :] * (GROUP - 1.0 - places[:, None]))
    query_scale = jnp.exp(-rates[None, :] * (places[:, None] + 1.0))
    group_decay = jnp.exp(-rates * GROUP)[:, None, None]
    blocks = LENGTH // GROUP

    def advance(state_now, block):
        query_block, key_block, value_block = block
        query_wide = query_block.astype(jnp.float32)
        key_wide = key_block.astype(jnp.float32)
        value_wide = value_block.astype(jnp.float32)
        scores = jnp.einsum('ihd,jhd->hij', query_wide, key_wide)
        weights = (scores * within).astype(jnp.bfloat16)
        inner_part = jnp.einsum('hij,jhd->ihd', weights.astype(jnp.float32), value_wide)
        carried_part = jnp.einsum('ihd,hde->ihe', query_wide * query_scale[:, :, None], state_now, precision=lax.Precision.HIGHEST)
        decayed = (key_wide * key_scale[:, :, None]).astype(jnp.bfloat16)
        local_state = jnp.einsum('jhd,jhe->hde', decayed.astype(jnp.float32), value_wide)
        return (group_decay * state_now + local_state, inner_part + carried_part)
    results = []
    for seq_id in range(SEQS):
        rotation = offsets[seq_id].astype(jnp.int32) * GROUP

        def ordered(source):
            return jnp.roll(source[seq_id], -rotation, axis=0).reshape(blocks, GROUP, HEADS, HEAD_DIM)
        start_state = jnp.zeros((HEADS, HEAD_DIM, HEAD_DIM), jnp.float32)
        final_state, attended = lax.scan(advance, start_state, (ordered(queries), ordered(keys), ordered(values)))
        attended = attended.reshape(LENGTH, FEATURES)
        inv_rms = lax.rsqrt(lax.optimization_barrier(jnp.mean(attended * attended, axis=-1, keepdims=True)) + epsilon)
        normed = (attended * inv_rms * norm_gain.astype(jnp.float32)).astype(jnp.bfloat16)
        results.append(jnp.roll(normed, rotation, axis=0))
    return jnp.stack(results)
```

```python
import functools

import jax
import jax.numpy as jnp
from jax import lax
from jax.experimental import pallas as pl
from jax.experimental.pallas import tpu as pltpu
from jax.sharding import PartitionSpec as P

epsilon = 1e-05
CHUNK = 256
LANES = 128
F32 = jnp.float32
BF16 = jnp.bfloat16
PARAMS = pltpu.CompilerParams(vmem_limit_bytes=16 * 2**20)


def dot(left, right, left_dim, right_dim):
    return lax.dot_general(
        left, right, (((left_dim,), (right_dim,)), ((), ())), preferred_element_type=F32
    )


def rows_of(shape):
    return lax.broadcasted_iota(jnp.int32, shape, 0).astype(F32)


def times_state(query, state):
    high = state.astype(BF16)
    low = (state - high.astype(F32)).astype(BF16)
    return dot(
        jnp.concatenate([query, query], axis=1), jnp.concatenate([high, low], axis=0), 1, 0
    )


def local_kernel(rate_ref, k_ref, v_ref, out_ref):
    rate = rate_ref[pl.program_id(0)]
    block_len, head_size = k_ref.shape
    places = rows_of((block_len, head_size))
    scale = jnp.exp(-rate * (block_len - 1.0 - places))
    decayed = (k_ref[...].astype(F32) * scale).astype(BF16)
    out_ref[0] = dot(decayed, v_ref[...], 0, 0)


def inner_kernel(rate_ref, q_ref, k_ref, v_ref, out_ref):
    rate = rate_ref[pl.program_id(0)]
    block_len, head_size = q_ref.shape
    chunk = min(CHUNK, block_len)
    square = (chunk, chunk)
    distance = rows_of(square) - lax.broadcasted_iota(jnp.int32, square, 1).astype(F32)
    within = jnp.where(distance >= 0.0, jnp.exp(-rate * jnp.maximum(distance, 0.0)), 0.0)
    places = rows_of((chunk, head_size))
    key_scale = jnp.exp(-rate * (chunk - 1.0 - places))
    query_scale = jnp.exp(-rate * (places + 1.0))
    chunk_decay = jnp.exp(jnp.full((head_size, head_size), -rate * chunk, F32))
    state = None
    for start in range(0, block_len, chunk):
        here = pl.ds(start, chunk)
        query, key, value = q_ref[here, :], k_ref[here, :], v_ref[here, :]
        weights = (dot(query, key, 1, 1) * within).astype(BF16)
        result = dot(weights, value, 1, 0)
        if state is not None:
            result = result + query_scale * times_state(query, state)
        out_ref[here, :] = result
        if start + chunk < block_len:
            decayed = (key.astype(F32) * key_scale).astype(BF16)
            added = dot(decayed, value, 0, 0)
            state = added if state is None else chunk_decay * state + added


def scan_kernel(block_len, rate_ref, place_ref, offset_ref, in_ref, out_ref):
    count, rows, lanes = in_ref.shape
    heads = rate_ref.shape[0]
    rate = rate_ref[place_ref[0] * heads // count]
    decay = jnp.exp(jnp.full((rows, lanes), -rate * block_len, F32))
    state = jnp.zeros((rows, lanes), F32)
    place = offset_ref[0]
    for _ in range(count):
        out_ref[place] = state
        state = decay * state + in_ref[place]
        place = jnp.where(place + 1 == count, 0, place + 1)


def attend_kernel(rate_ref, q_ref, inner_ref, state_ref, out_ref, square_ref):
    step = pl.program_id(0)
    rows, columns = q_ref.shape
    heads, head_size, _ = state_ref.shape
    places = rows_of((rows, head_size)) + (step * rows + 1).astype(F32)
    total = jnp.zeros((rows, head_size), F32)
    for head in range(heads):
        here = pl.ds(head * head_size, head_size)
        scale = jnp.exp(-rate_ref[head] * places)
        attended = inner_ref[:, here] + scale * times_state(q_ref[:, here], state_ref[head])
        out_ref[:, here] = attended
        total = total + attended * attended
    for part in range(rows // LANES):
        piece = total[part * LANES : (part + 1) * LANES]
        square_ref[0, part : part + 1, :] = jnp.sum(piece.T, axis=0, keepdims=True)


def norm_kernel(features_all, attended_ref, squares_ref, gain_ref, out_ref):
    rows = attended_ref.shape[0]
    total = jnp.sum(squares_ref[:, 0], axis=0)
    inv_rms = lax.rsqrt(total / features_all + epsilon)
    for part in range(rows // LANES):
        column = jnp.broadcast_to(inv_rms[part : part + 1], (LANES, LANES)).T[:, :1]
        here = pl.ds(part * LANES, LANES)
        out_ref[here, :] = (attended_ref[here, :] * column * gain_ref[...]).astype(BF16)


def body(queries, keys, values, decay_rate, norm_gain, offsets):
    seq_count, block_len, columns = queries.shape
    heads = decay_rate.shape[0]
    head_size = columns // heads
    seq_size = lax.axis_size("seq")
    head_parts = lax.axis_size("head")
    queries, keys, values = (x.reshape(block_len, columns) for x in (queries, keys, values))
    smem = pl.BlockSpec(memory_space=pltpu.SMEM)
    by_head = pl.BlockSpec((block_len, head_size), lambda h: (0, h))
    state_type = jax.ShapeDtypeStruct((heads, head_size, head_size), F32)
    wide_type = jax.ShapeDtypeStruct((block_len, columns), F32)

    local_state = pl.pallas_call(
        local_kernel,
        grid=(heads,),
        in_specs=[smem, by_head, by_head],
        out_specs=pl.BlockSpec((1, head_size, head_size), lambda h: (h, 0, 0)),
        out_shape=state_type,
        name="local_state",
        compiler_params=PARAMS,
        cost_estimate=pl.CostEstimate(
            flops=2 * block_len * columns * head_size,
            bytes_accessed=4 * block_len * columns + 4 * columns * head_size,
            transcendentals=block_len * columns,
        ),
    )(decay_rate, keys, values)

    piece_rows = columns // seq_size
    pieces = lax.all_to_all(
        local_state.reshape(seq_size, piece_rows, head_size), "seq", 0, 0, tiled=True
    )
    inner = pl.pallas_call(
        inner_kernel,
        grid=(heads,),
        in_specs=[smem, by_head, by_head, by_head],
        out_specs=by_head,
        out_shape=wide_type,
        name="inner",
        compiler_params=PARAMS,
        cost_estimate=pl.CostEstimate(
            flops=2 * block_len * columns * (2 * CHUNK + 3 * head_size),
            bytes_accessed=10 * block_len * columns,
            transcendentals=CHUNK * CHUNK * heads,
        ),
    )(decay_rate, queries, keys, values)

    place = lax.axis_index("seq").astype(jnp.int32).reshape(1)
    vmem = pl.BlockSpec(memory_space=pltpu.VMEM)
    prefixes = pl.pallas_call(
        functools.partial(scan_kernel, float(block_len)),
        in_specs=[smem, smem, smem, vmem],
        out_specs=vmem,
        out_shape=jax.ShapeDtypeStruct(pieces.shape, F32),
        name="scan",
        compiler_params=PARAMS,
    )(decay_rate, place, offsets, pieces)
    incoming = lax.all_to_all(prefixes, "seq", 0, 0, tiled=True).reshape(state_type.shape)

    steps = block_len // CHUNK
    by_rows = pl.BlockSpec((CHUNK, columns), lambda i: (i, 0))
    parts = CHUNK // LANES
    attended, squares = pl.pallas_call(
        attend_kernel,
        grid=(steps,),
        in_specs=[smem, by_rows, by_rows, pl.BlockSpec(state_type.shape, lambda i: (0, 0, 0))],
        out_specs=[by_rows, pl.BlockSpec((1, parts, LANES), lambda i: (i, 0, 0))],
        out_shape=[wide_type, jax.ShapeDtypeStruct((steps, parts, LANES), F32)],
        name="attend",
        compiler_params=PARAMS,
    )(decay_rate, queries, inner, incoming)

    squares = squares.reshape(1, block_len // LANES, LANES)
    gathered = lax.all_to_all(
        jnp.broadcast_to(squares, (head_parts, block_len // LANES, LANES)), "head", 0, 0, tiled=True
    )
    normed = pl.pallas_call(
        functools.partial(norm_kernel, float(columns * head_parts)),
        grid=(steps,),
        in_specs=[
            by_rows,
            pl.BlockSpec((head_parts, 1, parts, LANES), lambda i: (0, i, 0, 0)),
            pl.BlockSpec((1, columns), lambda i: (0, 0)),
        ],
        out_specs=by_rows,
        out_shape=jax.ShapeDtypeStruct((block_len, columns), BF16),
        name="norm",
        compiler_params=PARAMS,
    )(attended, gathered.reshape(head_parts, steps, parts, LANES), norm_gain.reshape(1, columns))
    return normed.reshape(seq_count, block_len, columns)


def solution(mesh):
    in_specs = (
        P(None, "seq", "head"),
        P(None, "seq", "head"),
        P(None, "seq", "head"),
        P("head"),
        P("head"),
        P(),
    )
    out_specs = P(None, "seq", "head")
    return jax.shard_map(body, mesh=mesh, in_specs=in_specs, out_specs=out_specs, check_vma=False)
```

```python
import functools

import jax
import jax.numpy as jnp
from jax import lax
from jax.experimental import pallas as pl
from jax.experimental.pallas import tpu as pltpu
from jax.sharding import PartitionSpec as P

epsilon = 1e-05
CHUNK = 256
LANES = 128
F32 = jnp.float32
BF16 = jnp.bfloat16
PARAMS = pltpu.CompilerParams(vmem_limit_bytes=16 * 2**20)


def dot(left, right, left_dim, right_dim):
    return lax.dot_general(
        left, right, (((left_dim,), (right_dim,)), ((), ())), preferred_element_type=F32
    )


def rows_of(shape):
    return lax.broadcasted_iota(jnp.int32, shape, 0).astype(F32)


def on_diagonal():
    square = (LANES, LANES)
    return lax.broadcasted_iota(jnp.int32, square, 0) == lax.broadcasted_iota(jnp.int32, square, 1)


def times_state(query, state):
    high = state.astype(BF16)
    low = (state - high.astype(F32)).astype(BF16)
    return dot(
        jnp.concatenate([query, query], axis=1), jnp.concatenate([high, low], axis=0), 1, 0
    )


def head_copies(refs, bufs, sems):
    heads, _, head_size = bufs[0].shape
    copies = []
    for head in range(heads):
        here = pl.ds(head * head_size, head_size)
        row = [
            pltpu.make_async_copy(ref.at[:, here], buf.at[head], sems.at[n, head])
            for n, (ref, buf) in enumerate(zip(refs, bufs))
        ]
        for copy in row:
            copy.start()
        copies.append(row)
    return copies


def local_kernel(rate_hbm, k_hbm, v_hbm, out_ref, rates, k_buf, v_buf, sems, rate_sem):
    rate_copy = pltpu.make_async_copy(rate_hbm, rates, rate_sem)
    rate_copy.start()
    copies = head_copies((k_hbm, v_hbm), (k_buf, v_buf), sems)
    heads, block_len, head_size = k_buf.shape
    chunk = min(CHUNK, block_len)
    places = rows_of((chunk, head_size))
    rate_copy.wait()
    for head in range(heads):
        rate = rates[head]
        scale = jnp.exp(-rate * (chunk - 1.0 - places))
        chunk_decay = jnp.exp(jnp.full((chunk, head_size), -rate * chunk, F32))
        for copy in copies[head]:
            copy.wait()
        pieces = []
        for start in reversed(range(0, block_len, chunk)):
            key = k_buf[head, start : start + chunk, :]
            pieces.append((key.astype(F32) * scale).astype(BF16))
            scale = scale * chunk_decay
        out_ref[head] = dot(jnp.concatenate(pieces[::-1], axis=0), v_buf[head], 0, 0)


def inner_kernel(
    rate_hbm, q_hbm, k_hbm, v_hbm, out_ref, query_ref, wide_ref,
    rates, q_buf, k_buf, v_buf, sems, rate_sem,
):
    rate_copy = pltpu.make_async_copy(rate_hbm, rates, rate_sem)
    rate_copy.start()
    copies = head_copies((q_hbm, k_hbm, v_hbm), (q_buf, k_buf, v_buf), sems)
    heads, block_len, head_size = q_buf.shape
    chunk = min(CHUNK, block_len)
    square = (chunk, chunk)
    distance = rows_of(square) - lax.broadcasted_iota(jnp.int32, square, 1).astype(F32)
    places = rows_of((chunk, head_size))
    rate_copy.wait()
    for head in range(heads):
        rate = rates[head]
        columns = pl.ds(head * head_size, head_size)
        within = jnp.where(distance >= 0.0, jnp.exp(-rate * jnp.maximum(distance, 0.0)), 0.0)
        key_scale = jnp.exp(-rate * (chunk - 1.0 - places))
        query_scale = jnp.exp(-rate * (places + 1.0))
        chunk_decay = jnp.exp(jnp.full((head_size, head_size), -rate * chunk, F32))
        wide_ref[head] = jnp.full(wide_ref.shape[1:], -rate, F32)
        for copy in copies[head]:
            copy.wait()
        state = None
        for start in range(0, block_len, chunk):
            here = pl.ds(start, chunk)
            query, key, value = q_buf[head, here, :], k_buf[head, here, :], v_buf[head, here, :]
            weights = (dot(query, key, 1, 1) * within).astype(BF16)
            result = dot(weights, value, 1, 0)
            if state is not None:
                result = result + query_scale * times_state(query, state)
            out_ref[here, columns] = result
            query_ref[here, columns] = query
            if start + chunk < block_len:
                decayed = (key.astype(F32) * key_scale).astype(BF16)
                added = dot(decayed, value, 0, 0)
                state = added if state is None else chunk_decay * state + added


def scan_kernel(block_len, wide_ref, offset_ref, in_ref, out_ref):
    count, rows, lanes = in_ref.shape
    heads = wide_ref.shape[0]
    decay = jnp.exp(wide_ref[lax.axis_index("seq") * heads // count] * block_len)
    state = jnp.zeros((rows, lanes), F32)
    place = offset_ref[0]
    for _ in range(count):
        out_ref[place] = state
        state = decay * state + in_ref[place]
        place = jnp.where(place + 1 == count, 0, place + 1)


def attend_kernel(query_ref, inner_ref, wide_ref, state_ref, out_ref, square_ref):
    heads, head_size, _ = state_ref.shape
    block_len = query_ref.shape[0]
    places = rows_of((LANES, head_size)) + 1.0
    states, scales, steps = [], [], []
    for head in range(heads):
        minus_rate = wide_ref[head, 0:1, :]
        scales.append(jnp.exp(minus_rate * places))
        steps.append(jnp.exp(minus_rate * LANES))
        state = state_ref[head]
        high = state.astype(BF16)
        low = (state - high.astype(F32)).astype(BF16)
        states.append(jnp.concatenate([high, low], axis=0))
    diagonal = on_diagonal()
    for start in range(0, block_len, LANES):
        here = pl.ds(start, LANES)
        total = jnp.zeros((LANES, head_size), F32)
        for head in range(heads):
            columns = pl.ds(head * head_size, head_size)
            query = query_ref[here, columns]
            carried = dot(jnp.concatenate([query, query], axis=1), states[head], 1, 0)
            attended = inner_ref[here, columns] + scales[head] * carried
            scales[head] = scales[head] * steps[head]
            out_ref[here, columns] = attended
            total = total + attended * attended
        sums = jnp.where(diagonal, jnp.sum(total, axis=1, keepdims=True), 0.0)
        square_ref[pl.ds(start // LANES, 1), :] = jnp.sum(sums, axis=0, keepdims=True)


def norm_kernel(features_all, attended_ref, squares_ref, gain_ref, out_hbm, out_buf, sems):
    inv_rms = lax.rsqrt(jnp.sum(squares_ref[...], axis=0) / features_all + epsilon)
    diagonal = on_diagonal()
    copies = []
    for part in range(inv_rms.shape[0]):
        column = jnp.sum(jnp.where(diagonal, inv_rms[part : part + 1], 0.0), axis=1, keepdims=True)
        here = pl.ds(part * LANES, LANES)
        out_buf[here, :] = (attended_ref[here, :] * column * gain_ref[...]).astype(BF16)
        copies.append(pltpu.make_async_copy(out_buf.at[here], out_hbm.at[here], sems.at[part]))
        copies[-1].start()
    for copy in copies:
        copy.wait()


def body(queries, keys, values, decay_rate, norm_gain, offsets):
    seq_count, block_len, columns = queries.shape
    heads = decay_rate.shape[0]
    head_size = columns // heads
    seq_size = lax.axis_size("seq")
    head_parts = lax.axis_size("head")
    queries, keys, values, decay_rate = (
        pltpu.with_memory_space_constraint(x, pltpu.HBM)
        for x in (*(x.reshape(block_len, columns) for x in (queries, keys, values)), decay_rate)
    )
    smem = pl.BlockSpec(memory_space=pltpu.SMEM)
    vmem = pl.BlockSpec(memory_space=pltpu.VMEM)
    hbm = pl.BlockSpec(memory_space=pltpu.HBM)
    state_type = jax.ShapeDtypeStruct((heads, head_size, head_size), F32)
    wide_type = jax.ShapeDtypeStruct((block_len, columns), F32)
    piece_rows = columns // seq_size
    parts = block_len // LANES
    buffer = pltpu.VMEM((heads, block_len, head_size), BF16)
    rates = pltpu.SMEM((heads,), F32)

    local_state = pl.pallas_call(
        local_kernel,
        in_specs=[hbm] * 3,
        out_specs=vmem,
        out_shape=state_type,
        scratch_shapes=[rates, buffer, buffer, pltpu.SemaphoreType.DMA((2, heads)), pltpu.SemaphoreType.DMA],
        name="local_state",
        compiler_params=PARAMS,
        cost_estimate=pl.CostEstimate(
            flops=2 * block_len * columns * head_size,
            bytes_accessed=4 * block_len * columns + 4 * columns * head_size,
            transcendentals=block_len * columns,
        ),
    )(decay_rate, keys, values)

    pieces = lax.all_to_all(
        local_state.reshape(seq_size, piece_rows, head_size), "seq", 0, 0, tiled=True
    )
    inner, query_copy, wide_rates = pl.pallas_call(
        inner_kernel,
        in_specs=[hbm] * 4,
        out_specs=[vmem] * 3,
        out_shape=[
            wide_type,
            jax.ShapeDtypeStruct((block_len, columns), BF16),
            jax.ShapeDtypeStruct((heads, piece_rows, head_size), F32),
        ],
        scratch_shapes=[
            rates, buffer, buffer, buffer, pltpu.SemaphoreType.DMA((3, heads)), pltpu.SemaphoreType.DMA,
        ],
        name="inner",
        compiler_params=PARAMS,
        cost_estimate=pl.CostEstimate(
            flops=2 * block_len * columns * (2 * CHUNK + 3 * head_size),
            bytes_accessed=16 * block_len * columns,
            transcendentals=CHUNK * CHUNK * heads,
        ),
    )(decay_rate, queries, keys, values)

    prefixes = pl.pallas_call(
        functools.partial(scan_kernel, float(block_len)),
        in_specs=[vmem, smem, vmem],
        out_specs=vmem,
        out_shape=jax.ShapeDtypeStruct(pieces.shape, F32),
        name="scan",
        compiler_params=PARAMS,
    )(wide_rates, offsets, pieces)
    incoming = lax.all_to_all(prefixes, "seq", 0, 0, tiled=True).reshape(state_type.shape)

    attended, squares = pl.pallas_call(
        attend_kernel,
        in_specs=[vmem] * 4,
        out_specs=[vmem] * 2,
        out_shape=[wide_type, jax.ShapeDtypeStruct((parts, LANES), F32)],
        name="attend",
        compiler_params=PARAMS,
    )(query_copy, inner, wide_rates, incoming)

    gathered = lax.all_to_all(
        jnp.broadcast_to(squares, (head_parts, parts, LANES)), "head", 0, 0, tiled=True
    )
    normed = pl.pallas_call(
        functools.partial(norm_kernel, float(columns * head_parts)),
        in_specs=[vmem] * 3,
        out_specs=hbm,
        out_shape=jax.ShapeDtypeStruct((block_len, columns), BF16),
        scratch_shapes=[pltpu.VMEM((block_len, columns), BF16), pltpu.SemaphoreType.DMA((parts,))],
        name="norm",
        compiler_params=PARAMS,
    )(attended, gathered, norm_gain.reshape(1, columns))
    return normed.reshape(seq_count, block_len, columns)


def solution(mesh):
    in_specs = (
        P(None, "seq", "head"),
        P(None, "seq", "head"),
        P(None, "seq", "head"),
        P("head"),
        P("head"),
        P(),
    )
    out_specs = P(None, "seq", "head")
    return jax.shard_map(body, mesh=mesh, in_specs=in_specs, out_specs=out_specs, check_vma=False)
```

```python
import functools

import jax
import jax.numpy as jnp
from jax import lax
from jax.experimental import pallas as pl
from jax.experimental.pallas import tpu as pltpu
from jax.sharding import PartitionSpec as P

epsilon = 1e-05
CHUNK = 256
LANES = 128
ROTATION = 10
F32 = jnp.float32
BF16 = jnp.bfloat16
PARAMS = pltpu.CompilerParams(vmem_limit_bytes=16 * 2**20)


def dot(left, right, left_dim, right_dim):
    return lax.dot_general(
        left, right, (((left_dim,), (right_dim,)), ((), ())), preferred_element_type=F32
    )


def rows_of(shape):
    return lax.broadcasted_iota(jnp.int32, shape, 0).astype(F32)


def on_diagonal():
    square = (LANES, LANES)
    return lax.broadcasted_iota(jnp.int32, square, 0) == lax.broadcasted_iota(jnp.int32, square, 1)


def times_state(query, state):
    high = state.astype(BF16)
    low = (state - high.astype(F32)).astype(BF16)
    return dot(
        jnp.concatenate([query, query], axis=1), jnp.concatenate([high, low], axis=0), 1, 0
    )


def head_copies(refs, bufs, sems):
    heads, _, head_size = bufs[0].shape
    copies = []
    for head in range(heads):
        here = pl.ds(head * head_size, head_size)
        row = [
            pltpu.make_async_copy(ref.at[:, here], buf.at[head], sems.at[n, head])
            for n, (ref, buf) in enumerate(zip(refs, bufs))
        ]
        for copy in row:
            copy.start()
        copies.append(row)
    return copies


def local_kernel(
    rate_hbm, k_hbm, v_hbm, out_hbm, rates, k_buf, v_buf, out_buf, sems, rate_sem, out_sems
):
    rate_copy = pltpu.make_async_copy(rate_hbm, rates, rate_sem)
    rate_copy.start()
    copies = head_copies((k_hbm, v_hbm), (k_buf, v_buf), sems)
    heads, block_len, head_size = k_buf.shape
    chunk = min(CHUNK, block_len)
    places = rows_of((chunk, head_size))
    rate_copy.wait()
    out_copies = []
    for head in range(heads):
        rate = rates[head]
        scale = jnp.exp(-rate * (chunk - 1.0 - places))
        chunk_decay = jnp.exp(jnp.full((chunk, head_size), -rate * chunk, F32))
        for copy in copies[head]:
            copy.wait()
        pieces = []
        for start in reversed(range(0, block_len, chunk)):
            key = k_buf[head, start : start + chunk, :]
            pieces.append((key.astype(F32) * scale).astype(BF16))
            scale = scale * chunk_decay
        out_buf[head] = dot(jnp.concatenate(pieces[::-1], axis=0), v_buf[head], 0, 0)
        out_copies.append(pltpu.make_async_copy(out_buf.at[head], out_hbm.at[head], out_sems.at[head]))
        out_copies[-1].start()
    for copy in out_copies:
        copy.wait()


def inner_kernel(
    rate_hbm, q_hbm, k_hbm, v_hbm, out_ref, query_ref, wide_ref,
    rates, q_buf, k_buf, v_buf, sems, rate_sem,
):
    rate_copy = pltpu.make_async_copy(rate_hbm, rates, rate_sem)
    rate_copy.start()
    copies = head_copies((q_hbm, k_hbm, v_hbm), (q_buf, k_buf, v_buf), sems)
    heads, block_len, head_size = q_buf.shape
    chunk = min(CHUNK, block_len)
    square = (chunk, chunk)
    distance = rows_of(square) - lax.broadcasted_iota(jnp.int32, square, 1).astype(F32)
    places = rows_of((chunk, head_size))
    rate_copy.wait()
    for head in range(heads):
        rate = rates[head]
        columns = pl.ds(head * head_size, head_size)
        within = jnp.where(distance >= 0.0, jnp.exp(-rate * jnp.maximum(distance, 0.0)), 0.0)
        key_scale = jnp.exp(-rate * (chunk - 1.0 - places))
        query_scale = jnp.exp(-rate * (places + 1.0))
        chunk_decay = jnp.exp(jnp.full((head_size, head_size), -rate * chunk, F32))
        wide_ref[head] = jnp.full(wide_ref.shape[1:], -rate, F32)
        for copy in copies[head]:
            copy.wait()
        state = None
        for start in range(0, block_len, chunk):
            here = pl.ds(start, chunk)
            query, key, value = q_buf[head, here, :], k_buf[head, here, :], v_buf[head, here, :]
            weights = (dot(query, key, 1, 1) * within).astype(BF16)
            result = dot(weights, value, 1, 0)
            if state is not None:
                result = result + query_scale * times_state(query, state)
            out_ref[here, columns] = result
            query_ref[here, columns] = query
            if start + chunk < block_len:
                decayed = (key.astype(F32) * key_scale).astype(BF16)
                added = dot(decayed, value, 0, 0)
                state = added if state is None else chunk_decay * state + added


def scan_kernel(block_len, wide_ref, offset_ref, in_ref, out_ref):
    count, rows, lanes = in_ref.shape
    heads = wide_ref.shape[0]
    mine = lax.rem(lax.axis_index("seq") + (count - ROTATION % count), count)
    decay = jnp.exp(wide_ref[mine * heads // count] * block_len)
    state = jnp.zeros((rows, lanes), F32)
    place = lax.rem(offset_ref[0] + (count - ROTATION % count), count)
    for _ in range(count):
        out_ref[place] = state
        state = decay * state + in_ref[place]
        place = jnp.where(place + 1 == count, 0, place + 1)


def attend_kernel(query_ref, inner_ref, wide_ref, state_ref, out_ref, square_ref):
    heads, head_size, _ = state_ref.shape
    block_len = query_ref.shape[0]
    places = rows_of((LANES, head_size)) + 1.0
    states, scales, steps = [], [], []
    for head in range(heads):
        minus_rate = wide_ref[head, 0:1, :]
        scales.append(jnp.exp(minus_rate * places))
        steps.append(jnp.exp(minus_rate * LANES))
        state = state_ref[head]
        high = state.astype(BF16)
        low = (state - high.astype(F32)).astype(BF16)
        states.append(jnp.concatenate([high, low], axis=0))
    diagonal = on_diagonal()
    for start in range(0, block_len, LANES):
        here = pl.ds(start, LANES)
        total = jnp.zeros((LANES, head_size), F32)
        for head in range(heads):
            columns = pl.ds(head * head_size, head_size)
            query = query_ref[here, columns]
            carried = dot(jnp.concatenate([query, query], axis=1), states[head], 1, 0)
            attended = inner_ref[here, columns] + scales[head] * carried
            scales[head] = scales[head] * steps[head]
            out_ref[here, columns] = attended
            total = total + attended * attended
        sums = jnp.where(diagonal, jnp.sum(total, axis=1, keepdims=True), 0.0)
        square_ref[pl.ds(start // LANES, 1), :] = jnp.sum(sums, axis=0, keepdims=True)


def norm_kernel(features_all, attended_ref, squares_ref, gain_ref, out_hbm, out_buf, sems):
    inv_rms = lax.rsqrt(jnp.sum(squares_ref[...], axis=0) / features_all + epsilon)
    diagonal = on_diagonal()
    copies = []
    for part in range(inv_rms.shape[0]):
        column = jnp.sum(jnp.where(diagonal, inv_rms[part : part + 1], 0.0), axis=1, keepdims=True)
        here = pl.ds(part * LANES, LANES)
        out_buf[here, :] = (attended_ref[here, :] * column * gain_ref[...]).astype(BF16)
        copies.append(pltpu.make_async_copy(out_buf.at[here], out_hbm.at[here], sems.at[part]))
        copies[-1].start()
    for copy in copies:
        copy.wait()


def body(queries, keys, values, decay_rate, norm_gain, offsets):
    seq_count, block_len, columns = queries.shape
    heads = decay_rate.shape[0]
    head_size = columns // heads
    seq_size = lax.axis_size("seq")
    head_parts = lax.axis_size("head")
    queries, keys, values, decay_rate = (
        pltpu.with_memory_space_constraint(x, pltpu.HBM)
        for x in (*(x.reshape(block_len, columns) for x in (queries, keys, values)), decay_rate)
    )
    smem = pl.BlockSpec(memory_space=pltpu.SMEM)
    vmem = pl.BlockSpec(memory_space=pltpu.VMEM)
    hbm = pl.BlockSpec(memory_space=pltpu.HBM)
    state_type = jax.ShapeDtypeStruct((heads, head_size, head_size), F32)
    wide_type = jax.ShapeDtypeStruct((block_len, columns), F32)
    piece_rows = columns // seq_size
    parts = block_len // LANES
    buffer = pltpu.VMEM((heads, block_len, head_size), BF16)
    rates = pltpu.SMEM((heads,), F32)

    dma = pltpu.SemaphoreType.DMA
    local_state = pl.pallas_call(
        local_kernel,
        in_specs=[hbm] * 3,
        out_specs=hbm,
        out_shape=state_type,
        scratch_shapes=[
            rates, buffer, buffer, pltpu.VMEM(state_type.shape, F32),
            dma((2, heads)), dma, dma((heads,)),
        ],
        name="local_state",
        compiler_params=PARAMS,
        cost_estimate=pl.CostEstimate(
            flops=2 * block_len * columns * head_size,
            bytes_accessed=4 * block_len * columns + 4 * columns * head_size,
            transcendentals=block_len * columns,
        ),
    )(decay_rate, keys, values)

    seq_order = [(i + ROTATION) % seq_size for i in range(seq_size)]
    head_order = [*range(0, head_parts, 2), *range(1, head_parts, 2)]

    def exchange(array):
        return lax.all_to_all(array, "seq", 0, 0, tiled=True, axis_index_groups=[seq_order])

    pieces = exchange(local_state.reshape(seq_size, piece_rows, head_size))
    inner, query_copy, wide_rates = pl.pallas_call(
        inner_kernel,
        in_specs=[hbm] * 4,
        out_specs=[vmem] * 3,
        out_shape=[
            wide_type,
            jax.ShapeDtypeStruct((block_len, columns), BF16),
            jax.ShapeDtypeStruct((heads, piece_rows, head_size), F32),
        ],
        scratch_shapes=[rates, buffer, buffer, buffer, dma((3, heads)), dma],
        name="inner",
        compiler_params=PARAMS,
        cost_estimate=pl.CostEstimate(
            flops=2 * block_len * columns * (2 * CHUNK + 3 * head_size),
            bytes_accessed=16 * block_len * columns,
            transcendentals=CHUNK * CHUNK * heads,
        ),
    )(decay_rate, queries, keys, values)

    prefixes = pl.pallas_call(
        functools.partial(scan_kernel, float(block_len)),
        in_specs=[vmem, smem, vmem],
        out_specs=vmem,
        out_shape=jax.ShapeDtypeStruct(pieces.shape, F32),
        name="scan",
        compiler_params=PARAMS,
    )(wide_rates, offsets, pieces)
    incoming = exchange(prefixes).reshape(state_type.shape)

    attended, squares = pl.pallas_call(
        attend_kernel,
        in_specs=[vmem] * 4,
        out_specs=[vmem] * 2,
        out_shape=[wide_type, jax.ShapeDtypeStruct((parts, LANES), F32)],
        name="attend",
        compiler_params=PARAMS,
    )(query_copy, inner, wide_rates, incoming)

    gathered = lax.all_to_all(
        jnp.broadcast_to(squares, (head_parts, parts, LANES)),
        "head",
        0,
        0,
        tiled=True,
        axis_index_groups=[head_order],
    )
    normed = pl.pallas_call(
        functools.partial(norm_kernel, float(columns * head_parts)),
        in_specs=[vmem] * 3,
        out_specs=hbm,
        out_shape=jax.ShapeDtypeStruct((block_len, columns), BF16),
        scratch_shapes=[pltpu.VMEM((block_len, columns), BF16), pltpu.SemaphoreType.DMA((parts,))],
        name="norm",
        compiler_params=PARAMS,
    )(attended, gathered, norm_gain.reshape(1, columns))
    return normed.reshape(seq_count, block_len, columns)


def solution(mesh):
    in_specs = (
        P(None, "seq", "head"),
        P(None, "seq", "head"),
        P(None, "seq", "head"),
        P("head"),
        P("head"),
        P(),
    )
    out_specs = P(None, "seq", "head")
    return jax.shard_map(body, mesh=mesh, in_specs=in_specs, out_specs=out_specs, check_vma=False)
```

```python
import functools

import jax
import jax.numpy as jnp
from jax import lax
from jax.experimental import pallas as pl
from jax.experimental.pallas import tpu as pltpu
from jax.sharding import PartitionSpec as P

epsilon = 1e-05
CHUNK = 256
LANES = 128
ROTATION = 21
HEAD_START = 10
F32 = jnp.float32
BF16 = jnp.bfloat16
PARAMS = pltpu.CompilerParams(vmem_limit_bytes=16 * 2**20)


def dot(left, right, left_dim, right_dim):
    return lax.dot_general(
        left, right, (((left_dim,), (right_dim,)), ((), ())), preferred_element_type=F32
    )


def rows_of(shape):
    return lax.broadcasted_iota(jnp.int32, shape, 0).astype(F32)


def on_diagonal():
    square = (LANES, LANES)
    return lax.broadcasted_iota(jnp.int32, square, 0) == lax.broadcasted_iota(jnp.int32, square, 1)


def times_state(query, state):
    high = state.astype(BF16)
    low = (state - high.astype(F32)).astype(BF16)
    return dot(
        jnp.concatenate([query, query], axis=1), jnp.concatenate([high, low], axis=0), 1, 0
    )


def head_copies(refs, bufs, sems):
    heads, _, head_size = bufs[0].shape
    copies = []
    for head in range(heads):
        here = pl.ds(head * head_size, head_size)
        row = [
            pltpu.make_async_copy(ref.at[:, here], buf.at[head], sems.at[n, head])
            for n, (ref, buf) in enumerate(zip(refs, bufs))
        ]
        for copy in row:
            copy.start()
        copies.append(row)
    return copies


def local_kernel(
    rate_hbm, k_hbm, v_hbm, out_hbm, rates, k_buf, v_buf, out_buf, sems, rate_sem, out_sems
):
    rate_copy = pltpu.make_async_copy(rate_hbm, rates, rate_sem)
    rate_copy.start()
    copies = head_copies((k_hbm, v_hbm), (k_buf, v_buf), sems)
    heads, block_len, head_size = k_buf.shape
    chunk = min(CHUNK, block_len)
    places = rows_of((chunk, head_size))
    rate_copy.wait()
    out_copies = []
    for head in range(heads):
        rate = rates[head]
        scale = jnp.exp(-rate * (chunk - 1.0 - places))
        chunk_decay = jnp.exp(jnp.full((chunk, head_size), -rate * chunk, F32))
        for copy in copies[head]:
            copy.wait()
        pieces = []
        for start in reversed(range(0, block_len, chunk)):
            key = k_buf[head, start : start + chunk, :]
            pieces.append((key.astype(F32) * scale).astype(BF16))
            scale = scale * chunk_decay
        out_buf[head] = dot(jnp.concatenate(pieces[::-1], axis=0), v_buf[head], 0, 0)
        out_copies.append(pltpu.make_async_copy(out_buf.at[head], out_hbm.at[head], out_sems.at[head]))
        out_copies[-1].start()
    for copy in out_copies:
        copy.wait()


def inner_kernel(
    rate_hbm, q_hbm, k_hbm, v_hbm, out_ref, query_ref, wide_ref,
    rates, q_buf, k_buf, v_buf, sems, rate_sem,
):
    rate_copy = pltpu.make_async_copy(rate_hbm, rates, rate_sem)
    rate_copy.start()
    copies = head_copies((q_hbm, k_hbm, v_hbm), (q_buf, k_buf, v_buf), sems)
    heads, block_len, head_size = q_buf.shape
    chunk = min(CHUNK, block_len)
    square = (chunk, chunk)
    distance = rows_of(square) - lax.broadcasted_iota(jnp.int32, square, 1).astype(F32)
    places = rows_of((chunk, head_size))
    rate_copy.wait()
    for head in range(heads):
        rate = rates[head]
        columns = pl.ds(head * head_size, head_size)
        within = jnp.where(distance >= 0.0, jnp.exp(-rate * jnp.maximum(distance, 0.0)), 0.0)
        key_scale = jnp.exp(-rate * (chunk - 1.0 - places))
        query_scale = jnp.exp(-rate * (places + 1.0))
        chunk_decay = jnp.exp(jnp.full((head_size, head_size), -rate * chunk, F32))
        wide_ref[head] = jnp.full(wide_ref.shape[1:], -rate, F32)
        for copy in copies[head]:
            copy.wait()
        state = None
        for start in range(0, block_len, chunk):
            here = pl.ds(start, chunk)
            query, key, value = q_buf[head, here, :], k_buf[head, here, :], v_buf[head, here, :]
            weights = (dot(query, key, 1, 1) * within).astype(BF16)
            result = dot(weights, value, 1, 0)
            if state is not None:
                result = result + query_scale * times_state(query, state)
            out_ref[here, columns] = result
            query_ref[here, columns] = query
            if start + chunk < block_len:
                decayed = (key.astype(F32) * key_scale).astype(BF16)
                added = dot(decayed, value, 0, 0)
                state = added if state is None else chunk_decay * state + added


def scan_kernel(block_len, wide_ref, offset_ref, in_ref, out_ref):
    count, rows, lanes = in_ref.shape
    heads = wide_ref.shape[0]
    mine = lax.rem(lax.axis_index("seq") + (count - ROTATION % count), count)
    decay = jnp.exp(wide_ref[mine * heads // count] * block_len)
    state = jnp.zeros((rows, lanes), F32)
    place = lax.rem(offset_ref[0] + (count - ROTATION % count), count)
    for _ in range(count):
        out_ref[place] = state
        state = decay * state + in_ref[place]
        place = jnp.where(place + 1 == count, 0, place + 1)


def attend_kernel(query_ref, inner_ref, wide_ref, state_ref, out_ref, square_ref):
    heads, head_size, _ = state_ref.shape
    block_len = query_ref.shape[0]
    places = rows_of((LANES, head_size)) + 1.0
    states, scales, steps = [], [], []
    for head in range(heads):
        minus_rate = wide_ref[head, 0:1, :]
        scales.append(jnp.exp(minus_rate * places))
        steps.append(jnp.exp(minus_rate * LANES))
        state = state_ref[head]
        high = state.astype(BF16)
        low = (state - high.astype(F32)).astype(BF16)
        states.append(jnp.concatenate([high, low], axis=0))
    diagonal = on_diagonal()
    for start in range(0, block_len, LANES):
        here = pl.ds(start, LANES)
        total = jnp.zeros((LANES, head_size), F32)
        for head in range(heads):
            columns = pl.ds(head * head_size, head_size)
            query = query_ref[here, columns]
            carried = dot(jnp.concatenate([query, query], axis=1), states[head], 1, 0)
            attended = inner_ref[here, columns] + scales[head] * carried
            scales[head] = scales[head] * steps[head]
            out_ref[here, columns] = attended
            total = total + attended * attended
        sums = jnp.where(diagonal, jnp.sum(total, axis=1, keepdims=True), 0.0)
        square_ref[pl.ds(start // LANES, 1), :] = jnp.sum(sums, axis=0, keepdims=True)


def norm_kernel(features_all, attended_ref, squares_ref, gain_ref, out_hbm, out_buf, sems):
    inv_rms = lax.rsqrt(jnp.sum(squares_ref[...], axis=0) / features_all + epsilon)
    diagonal = on_diagonal()
    copies = []
    for part in range(inv_rms.shape[0]):
        column = jnp.sum(jnp.where(diagonal, inv_rms[part : part + 1], 0.0), axis=1, keepdims=True)
        here = pl.ds(part * LANES, LANES)
        out_buf[here, :] = (attended_ref[here, :] * column * gain_ref[...]).astype(BF16)
        copies.append(pltpu.make_async_copy(out_buf.at[here], out_hbm.at[here], sems.at[part]))
        copies[-1].start()
    for copy in copies:
        copy.wait()


def body(queries, keys, values, decay_rate, norm_gain, offsets):
    seq_count, block_len, columns = queries.shape
    heads = decay_rate.shape[0]
    head_size = columns // heads
    seq_size = lax.axis_size("seq")
    head_parts = lax.axis_size("head")
    queries, keys, values, decay_rate = (
        pltpu.with_memory_space_constraint(x, pltpu.HBM)
        for x in (*(x.reshape(block_len, columns) for x in (queries, keys, values)), decay_rate)
    )
    smem = pl.BlockSpec(memory_space=pltpu.SMEM)
    vmem = pl.BlockSpec(memory_space=pltpu.VMEM)
    hbm = pl.BlockSpec(memory_space=pltpu.HBM)
    state_type = jax.ShapeDtypeStruct((heads, head_size, head_size), F32)
    wide_type = jax.ShapeDtypeStruct((block_len, columns), F32)
    piece_rows = columns // seq_size
    parts = block_len // LANES
    buffer = pltpu.VMEM((heads, block_len, head_size), BF16)
    rates = pltpu.SMEM((heads,), F32)

    dma = pltpu.SemaphoreType.DMA
    local_state = pl.pallas_call(
        local_kernel,
        in_specs=[hbm] * 3,
        out_specs=hbm,
        out_shape=state_type,
        scratch_shapes=[
            rates, buffer, buffer, pltpu.VMEM(state_type.shape, F32),
            dma((2, heads)), dma, dma((heads,)),
        ],
        name="local_state",
        compiler_params=PARAMS,
        cost_estimate=pl.CostEstimate(
            flops=2 * block_len * columns * head_size,
            bytes_accessed=4 * block_len * columns + 4 * columns * head_size,
            transcendentals=block_len * columns,
        ),
    )(decay_rate, keys, values)

    seq_order = [(i + ROTATION) % seq_size for i in range(seq_size)]
    half = head_parts // 2
    head_order = [
        (HEAD_START + 2 * k) % head_parts + part for part in (1, 0) for k in range(half)
    ]

    def exchange(array):
        return lax.all_to_all(array, "seq", 0, 0, tiled=True, axis_index_groups=[seq_order])

    pieces = exchange(local_state.reshape(seq_size, piece_rows, head_size))
    inner, query_copy, wide_rates = pl.pallas_call(
        inner_kernel,
        in_specs=[hbm] * 4,
        out_specs=[vmem] * 3,
        out_shape=[
            wide_type,
            jax.ShapeDtypeStruct((block_len, columns), BF16),
            jax.ShapeDtypeStruct((heads, piece_rows, head_size), F32),
        ],
        scratch_shapes=[rates, buffer, buffer, buffer, dma((3, heads)), dma],
        name="inner",
        compiler_params=PARAMS,
        cost_estimate=pl.CostEstimate(
            flops=2 * block_len * columns * (2 * CHUNK + 3 * head_size),
            bytes_accessed=16 * block_len * columns,
            transcendentals=CHUNK * CHUNK * heads,
        ),
    )(decay_rate, queries, keys, values)

    prefixes = pl.pallas_call(
        functools.partial(scan_kernel, float(block_len)),
        in_specs=[vmem, smem, vmem],
        out_specs=vmem,
        out_shape=jax.ShapeDtypeStruct(pieces.shape, F32),
        name="scan",
        compiler_params=PARAMS,
    )(wide_rates, offsets, pieces)
    incoming = exchange(prefixes).reshape(state_type.shape)

    attended, squares = pl.pallas_call(
        attend_kernel,
        in_specs=[vmem] * 4,
        out_specs=[vmem] * 2,
        out_shape=[wide_type, jax.ShapeDtypeStruct((parts, LANES), F32)],
        name="attend",
        compiler_params=PARAMS,
    )(query_copy, inner, wide_rates, incoming)

    gathered = lax.all_to_all(
        jnp.broadcast_to(squares, (head_parts, parts, LANES)),
        "head",
        0,
        0,
        tiled=True,
        axis_index_groups=[head_order],
    )
    normed = pl.pallas_call(
        functools.partial(norm_kernel, float(columns * head_parts)),
        in_specs=[vmem] * 3,
        out_specs=hbm,
        out_shape=jax.ShapeDtypeStruct((block_len, columns), BF16),
        scratch_shapes=[pltpu.VMEM((block_len, columns), BF16), pltpu.SemaphoreType.DMA((parts,))],
        name="norm",
        compiler_params=PARAMS,
    )(attended, gathered, norm_gain.reshape(1, columns))
    return normed.reshape(seq_count, block_len, columns)


def solution(mesh):
    in_specs = (
        P(None, "seq", "head"),
        P(None, "seq", "head"),
        P(None, "seq", "head"),
        P("head"),
        P("head"),
        P(),
    )
    out_specs = P(None, "seq", "head")
    return jax.shard_map(body, mesh=mesh, in_specs=in_specs, out_specs=out_specs, check_vma=False)
```

```python
import functools

import jax
import jax.numpy as jnp
from jax import lax
from jax.experimental import pallas as pl
from jax.experimental.pallas import tpu as pltpu
from jax.sharding import PartitionSpec as P

epsilon = 1e-05
CHUNK = 256
LANES = 128
ROTATION = 21
HEAD_START = 10
F32 = jnp.float32
BF16 = jnp.bfloat16
PARAMS = pltpu.CompilerParams(vmem_limit_bytes=16 * 2**20)


def dot(left, right, left_dim, right_dim):
    return lax.dot_general(
        left, right, (((left_dim,), (right_dim,)), ((), ())), preferred_element_type=F32
    )


def rows_of(shape):
    return lax.broadcasted_iota(jnp.int32, shape, 0).astype(F32)


def on_diagonal():
    square = (LANES, LANES)
    return lax.broadcasted_iota(jnp.int32, square, 0) == lax.broadcasted_iota(jnp.int32, square, 1)


def times_state(query, state):
    high = state.astype(BF16)
    low = (state - high.astype(F32)).astype(BF16)
    return dot(
        jnp.concatenate([query, query], axis=1), jnp.concatenate([high, low], axis=0), 1, 0
    )


def head_copies(refs, bufs, sems):
    heads, _, head_size = bufs[0].shape
    copies = []
    for head in range(heads):
        here = pl.ds(head * head_size, head_size)
        row = [
            pltpu.make_async_copy(ref.at[:, here], buf.at[head], sems.at[n, head])
            for n, (ref, buf) in enumerate(zip(refs, bufs))
        ]
        for copy in row:
            copy.start()
        copies.append(row)
    return copies


def local_kernel(
    rate_hbm, k_hbm, v_hbm, out_ref, wide_ref, rates, k_buf, v_buf, sems, rate_sem
):
    rate_copy = pltpu.make_async_copy(rate_hbm, rates, rate_sem)
    rate_copy.start()
    copies = head_copies((k_hbm, v_hbm), (k_buf, v_buf), sems)
    heads, block_len, head_size = k_buf.shape
    chunk = min(CHUNK, block_len)
    places = rows_of((chunk, head_size))
    rate_copy.wait()
    for head in range(heads):
        rate = rates[head]
        wide_ref[head] = jnp.full(wide_ref.shape[1:], -rate, F32)
        scale = jnp.exp(-rate * (chunk - 1.0 - places))
        chunk_decay = jnp.exp(jnp.full((chunk, head_size), -rate * chunk, F32))
        for copy in copies[head]:
            copy.wait()
        pieces = []
        for start in reversed(range(0, block_len, chunk)):
            key = k_buf[head, start : start + chunk, :]
            pieces.append((key.astype(F32) * scale).astype(BF16))
            scale = scale * chunk_decay
        out_ref[head] = dot(jnp.concatenate(pieces[::-1], axis=0), v_buf[head], 0, 0)


def inner_kernel(
    rate_hbm, q_hbm, k_hbm, v_hbm, after, out_ref, query_ref,
    rates, q_buf, k_buf, v_buf, sems, rate_sem,
):
    rate_copy = pltpu.make_async_copy(rate_hbm, rates, rate_sem)
    rate_copy.start()
    copies = head_copies((q_hbm, k_hbm, v_hbm), (q_buf, k_buf, v_buf), sems)
    heads, block_len, head_size = q_buf.shape
    chunk = min(CHUNK, block_len)
    square = (chunk, chunk)
    distance = rows_of(square) - lax.broadcasted_iota(jnp.int32, square, 1).astype(F32)
    places = rows_of((chunk, head_size))
    rate_copy.wait()
    for head in range(heads):
        rate = rates[head]
        columns = pl.ds(head * head_size, head_size)
        within = jnp.where(distance >= 0.0, jnp.exp(-rate * jnp.maximum(distance, 0.0)), 0.0)
        key_scale = jnp.exp(-rate * (chunk - 1.0 - places))
        query_scale = jnp.exp(-rate * (places + 1.0))
        chunk_decay = jnp.exp(jnp.full((head_size, head_size), -rate * chunk, F32))
        for copy in copies[head]:
            copy.wait()
        state = None
        for start in range(0, block_len, chunk):
            here = pl.ds(start, chunk)
            query, key, value = q_buf[head, here, :], k_buf[head, here, :], v_buf[head, here, :]
            weights = (dot(query, key, 1, 1) * within).astype(BF16)
            result = dot(weights, value, 1, 0)
            if state is not None:
                result = result + query_scale * times_state(query, state)
            out_ref[here, columns] = result
            query_ref[here, columns] = query
            if start + chunk < block_len:
                decayed = (key.astype(F32) * key_scale).astype(BF16)
                added = dot(decayed, value, 0, 0)
                state = added if state is None else chunk_decay * state + added


def scan_kernel(block_len, wide_ref, offset_ref, in_ref, out_ref):
    count, rows, lanes = in_ref.shape
    heads = wide_ref.shape[0]
    mine = lax.rem(lax.axis_index("seq") + (count - ROTATION % count), count)
    decay = jnp.exp(wide_ref[mine * heads // count] * block_len)
    state = jnp.zeros((rows, lanes), F32)
    place = lax.rem(offset_ref[0] + (count - ROTATION % count), count)
    for _ in range(count):
        out_ref[place] = state
        state = decay * state + in_ref[place]
        place = jnp.where(place + 1 == count, 0, place + 1)


def attend_kernel(query_ref, inner_ref, wide_ref, state_ref, out_ref, square_ref):
    heads, head_size, _ = state_ref.shape
    block_len = query_ref.shape[0]
    places = rows_of((LANES, head_size)) + 1.0
    states, scales, steps = [], [], []
    for head in range(heads):
        minus_rate = wide_ref[head, 0:1, :]
        scales.append(jnp.exp(minus_rate * places))
        steps.append(jnp.exp(minus_rate * LANES))
        state = state_ref[head]
        high = state.astype(BF16)
        low = (state - high.astype(F32)).astype(BF16)
        states.append(jnp.concatenate([high, low], axis=0))
    diagonal = on_diagonal()
    for start in range(0, block_len, LANES):
        here = pl.ds(start, LANES)
        total = jnp.zeros((LANES, head_size), F32)
        for head in range(heads):
            columns = pl.ds(head * head_size, head_size)
            query = query_ref[here, columns]
            carried = dot(jnp.concatenate([query, query], axis=1), states[head], 1, 0)
            attended = inner_ref[here, columns] + scales[head] * carried
            scales[head] = scales[head] * steps[head]
            out_ref[here, columns] = attended
            total = total + attended * attended
        sums = jnp.where(diagonal, jnp.sum(total, axis=1, keepdims=True), 0.0)
        square_ref[pl.ds(start // LANES, 1), :] = jnp.sum(sums, axis=0, keepdims=True)


def norm_kernel(features_all, attended_ref, squares_ref, gain_ref, out_hbm, out_buf, sems):
    inv_rms = lax.rsqrt(jnp.sum(squares_ref[...], axis=0) / features_all + epsilon)
    diagonal = on_diagonal()
    copies = []
    for part in range(inv_rms.shape[0]):
        column = jnp.sum(jnp.where(diagonal, inv_rms[part : part + 1], 0.0), axis=1, keepdims=True)
        here = pl.ds(part * LANES, LANES)
        out_buf[here, :] = (attended_ref[here, :] * column * gain_ref[...]).astype(BF16)
        copies.append(pltpu.make_async_copy(out_buf.at[here], out_hbm.at[here], sems.at[part]))
        copies[-1].start()
    for copy in copies:
        copy.wait()


def body(queries, keys, values, decay_rate, norm_gain, offsets):
    seq_count, block_len, columns = queries.shape
    heads = decay_rate.shape[0]
    head_size = columns // heads
    seq_size = lax.axis_size("seq")
    head_parts = lax.axis_size("head")
    queries, keys, values, decay_rate = (
        pltpu.with_memory_space_constraint(x, pltpu.HBM)
        for x in (*(x.reshape(block_len, columns) for x in (queries, keys, values)), decay_rate)
    )
    smem = pl.BlockSpec(memory_space=pltpu.SMEM)
    vmem = pl.BlockSpec(memory_space=pltpu.VMEM)
    hbm = pl.BlockSpec(memory_space=pltpu.HBM)
    state_type = jax.ShapeDtypeStruct((heads, head_size, head_size), F32)
    wide_type = jax.ShapeDtypeStruct((block_len, columns), F32)
    piece_rows = columns // seq_size
    parts = block_len // LANES
    buffer = pltpu.VMEM((heads, block_len, head_size), BF16)
    rates = pltpu.SMEM((heads,), F32)

    dma = pltpu.SemaphoreType.DMA
    wide_type_rates = jax.ShapeDtypeStruct((heads, piece_rows, head_size), F32)
    local_state, wide_rates = pl.pallas_call(
        local_kernel,
        in_specs=[hbm] * 3,
        out_specs=[vmem, vmem],
        out_shape=[state_type, wide_type_rates],
        scratch_shapes=[rates, buffer, buffer, dma((2, heads)), dma],
        name="local_state",
        compiler_params=PARAMS,
        cost_estimate=pl.CostEstimate(
            flops=2 * block_len * columns * head_size,
            bytes_accessed=4 * block_len * columns + 4 * columns * head_size,
            transcendentals=block_len * columns,
        ),
    )(decay_rate, keys, values)

    seq_order = [(i + ROTATION) % seq_size for i in range(seq_size)]
    half = head_parts // 2
    head_order = [
        (HEAD_START + 2 * k) % head_parts + part for part in (1, 0) for k in range(half)
    ]

    def exchange(array):
        return lax.all_to_all(array, "seq", 0, 0, tiled=True, axis_index_groups=[seq_order])

    pieces = exchange(local_state.reshape(seq_size, piece_rows, head_size))
    prefixes = pl.pallas_call(
        functools.partial(scan_kernel, float(block_len)),
        in_specs=[vmem, smem, vmem],
        out_specs=vmem,
        out_shape=jax.ShapeDtypeStruct(pieces.shape, F32),
        name="scan",
        compiler_params=PARAMS,
    )(wide_rates, offsets, pieces)
    inner, query_copy = pl.pallas_call(
        inner_kernel,
        in_specs=[hbm] * 4 + [pl.BlockSpec(memory_space=pl.ANY)],
        out_specs=[vmem] * 2,
        out_shape=[
            wide_type,
            jax.ShapeDtypeStruct((block_len, columns), BF16),
        ],
        scratch_shapes=[rates, buffer, buffer, buffer, dma((3, heads)), dma],
        name="inner",
        compiler_params=PARAMS,
        cost_estimate=pl.CostEstimate(
            flops=2 * block_len * columns * (2 * CHUNK + 3 * head_size),
            bytes_accessed=16 * block_len * columns,
            transcendentals=CHUNK * CHUNK * heads,
        ),
    )(decay_rate, queries, keys, values, prefixes)

    incoming = exchange(prefixes).reshape(state_type.shape)

    attended, squares = pl.pallas_call(
        attend_kernel,
        in_specs=[vmem] * 4,
        out_specs=[vmem] * 2,
        out_shape=[wide_type, jax.ShapeDtypeStruct((parts, LANES), F32)],
        name="attend",
        compiler_params=PARAMS,
    )(query_copy, inner, wide_rates, incoming)

    gathered = lax.all_to_all(
        jnp.broadcast_to(squares, (head_parts, parts, LANES)),
        "head",
        0,
        0,
        tiled=True,
        axis_index_groups=[head_order],
    )
    normed = pl.pallas_call(
        functools.partial(norm_kernel, float(columns * head_parts)),
        in_specs=[vmem] * 3,
        out_specs=hbm,
        out_shape=jax.ShapeDtypeStruct((block_len, columns), BF16),
        scratch_shapes=[pltpu.VMEM((block_len, columns), BF16), pltpu.SemaphoreType.DMA((parts,))],
        name="norm",
        compiler_params=PARAMS,
    )(attended, gathered, norm_gain.reshape(1, columns))
    return normed.reshape(seq_count, block_len, columns)


def solution(mesh):
    in_specs = (
        P(None, "seq", "head"),
        P(None, "seq", "head"),
        P(None, "seq", "head"),
        P("head"),
        P("head"),
        P(),
    )
    out_specs = P(None, "seq", "head")
    return jax.shard_map(body, mesh=mesh, in_specs=in_specs, out_specs=out_specs, check_vma=False)
```
